32 devices in a mesh: chan: 2 (over core), face: 4 (over y, x), tile: 4 (over z).
Axes of the slice: x: 2, y: 2, z: 4, core: 2. Of those that a mesh axis runs over, the one named last changes fastest.
Arguments:
- field: bfloat16 [1, 128, 32, 4096], P(None, 'chan', 'tile', 'face'), may hold values from -6 to 6
- conv_weight: bfloat16 [3, 3, 128, 128], replicated, may hold values from -0.1875 to 0.1875
- order_map: int32 [2048], replicated, may hold values from 0 to 2047, each once
- legendre: bfloat16 [2048, 32, 2048], P(('chan', 'face', 'tile')), may hold values from -0.015625 to 0.015625
- spectral_weight: bfloat16 [2048, 128, 128], P(('face', 'tile')), may hold values from -0.5 to 0.5
Outputs:
- spectrum: bfloat16 [2048, 2, 1, 2048, 128], P('chan', None, None, ('face', 'tile'))
The draws below stay inside these ranges and needn't reach their ends.
Inputs may be any that keep to these rules, and one draw needn't show every extreme that they name: `order_map`: a permutation of the orders 0 to 2047.
All inputs are finite; a program needn't handle non-finite values.
Results may differ from the reference program's by a relative error of at most 0.013.
Values may be sent and summed in bfloat16 or wider, within the bound.
No kernel may reach another device: no remote copies, remote signals or barrier semaphores. Data moves between devices by JAX's collectives and lax.ppermute only.
A program may use at most 320 MiB of HBM per device.

```python
import math
import jax
import jax.numpy as jnp
from jax import lax

CHANNELS = 128
PIXELS = 4096
DEGREES = 2048
SAMPLES = 1
CYCLES = 32


def steps_of(rng, extent, pieces, smallest, top_value):
    def one(position, shards_of):
        heights = jax.random.uniform(jax.random.fold_in(jax.random.fold_in(rng, 6), position), (shards_of,), jnp.float32, smallest / len(pieces), top_value / len(pieces))
        return jnp.repeat(jnp.exp(heights), extent[position] // shards_of).reshape((-1,) + (1,) * (len(extent) - position - 1))

    gain = one(*pieces[0])
    for cut in pieces[1:]:
        gain = gain * one(*cut)
    return gain


def gaussian(key, extent, scale, most, split=(), kind=jnp.bfloat16):
    entries = jax.random.normal(key, extent, jnp.float32) * scale
    if len(split) > 0:
        entries = steps_of(key, extent, split, -0.22, 0.18) * entries
    return jnp.clip(entries, min=-most, max=most).astype(kind)


def setup_inputs(seed: int = 0) -> dict:
    key_list = jax.random.split(jax.random.key(seed), 6)
    field = gaussian(key_list[0], (SAMPLES, CHANNELS, CYCLES, PIXELS), 1.0, 6.0, ((1, 2), (2, 4), (3, 4)))
    conv_weight = gaussian(key_list[1], (3, 3, CHANNELS, CHANNELS), (9 * CHANNELS) ** -0.5, 0.1875)
    order_map = jax.random.permutation(key_list[2], DEGREES).astype(jnp.int32)
    legendre = gaussian(key_list[3], (DEGREES, CYCLES, DEGREES), (CYCLES * PIXELS) ** -0.5, 0.015625, ((0, 32),))
    spectral_weight = gaussian(key_list[4], (DEGREES, CHANNELS, CHANNELS), CHANNELS ** -0.5, 0.5, ((0, 16),))
    return dict(field=field, conv_weight=conv_weight, order_map=order_map, legendre=legendre, spectral_weight=spectral_weight)


def reference(field, conv_weight, order_map, legendre, spectral_weight):
    padded = jnp.pad(field, ((0, 0), (0, 0), (1, 1), (0, 0)))
    padded = jnp.concatenate([padded[:, :, :, -1:], padded, padded[:, :, :, :1]], axis=3)
    summed = jnp.zeros((SAMPLES, CHANNELS, CYCLES, PIXELS), jnp.float32)
    for shift_r in range(3):
        for shift_p in range(3):
            window = padded[:, :, shift_r:shift_r + CYCLES, shift_p:shift_p + PIXELS].astype(jnp.float32)
            summed = summed + jnp.einsum("birp,io->borp", window, conv_weight[shift_r, shift_p].astype(jnp.float32))
    hidden = summed.astype(jnp.bfloat16)
    fourier = jnp.fft.fft(hidden.astype(jnp.float32), axis=3)
    picked = jnp.take(fourier, order_map % PIXELS, axis=3)
    parity = (jnp.arange(CYCLES, dtype=jnp.int32) % 2).astype(jnp.int32)
    turns = (order_map[None, :] * parity[:, None]) % (2 * PIXELS)
    angle = turns.astype(jnp.float32) * jnp.float32(-math.pi / PIXELS)
    rotated_re = jnp.real(picked) * jnp.cos(angle) - jnp.imag(picked) * jnp.sin(angle)
    rotated_im = jnp.real(picked) * jnp.sin(angle) + jnp.imag(picked) * jnp.cos(angle)
    coeff = jnp.stack([rotated_re, rotated_im], axis=0).astype(jnp.bfloat16)
    cycle_rows = jnp.transpose(coeff, (4, 0, 1, 2, 3)).reshape(DEGREES // 64, 64, 2 * SAMPLES * CHANNELS, CYCLES)
    tables = legendre.reshape(DEGREES // 64, 64, CYCLES, DEGREES)
    orders_block = order_map.reshape(DEGREES // 64, 64)
    degree_ids = jnp.arange(DEGREES, dtype=jnp.int32)
    mixing = spectral_weight.astype(jnp.float32)

    def one_block(items):
        block_rows, block_table, block_orders = items
        assoc = jnp.einsum("kxr,krl->kxl", block_rows.astype(jnp.float32), block_table.astype(jnp.float32))
        keep = degree_ids[None, :] >= block_orders[:, None]
        assoc = jnp.where(keep[:, None, :], assoc, jnp.zeros_like(assoc)).astype(jnp.bfloat16)
        assoc = assoc.reshape(64, 2, SAMPLES, CHANNELS, DEGREES)
        mixed = jnp.einsum("kzbil,lio->kzblo", assoc.astype(jnp.float32), mixing)
        return mixed.astype(jnp.bfloat16)

    result = lax.map(one_block, (cycle_rows, tables, orders_block))
    return result.reshape(DEGREES, 2, SAMPLES, DEGREES, CHANNELS)
```

```python
import functools
import math

import jax
import jax.numpy as jnp
from jax import lax
from jax.experimental import pallas as pl
from jax.experimental.pallas import tpu as pltpu
from jax.sharding import PartitionSpec as P

LANES = 128
ROWS = 8


def extended(x, sides, width):
    for axis, dim in sides:
        count, length = (lax.axis_size(axis), x.shape[dim])
        up = [(i, (i + 1) % count) for i in range(count)]
        down = [(j, i) for i, j in up]
        last = lax.slice_in_dim(x, length - width, length, axis=dim)
        first = lax.slice_in_dim(x, 0, width, axis=dim)
        before = lax.ppermute(last, axis, up)
        after = lax.ppermute(first, axis, down)
        x = jnp.concatenate([before, x, after], axis=dim)
    return x


def stencil(padded, weights, cycle_count, pix_count):
    summed = None
    for shift_r in range(3):
        for shift_p in range(3):
            window = padded[:, :, shift_r : shift_r + cycle_count, shift_p : shift_p + pix_count]
            contrib = jnp.einsum(
                "birp,io->borp",
                window,
                weights[shift_r, shift_p],
                preferred_element_type=jnp.float32,
            )
            summed = contrib if summed is None else summed + contrib
    return summed


def clear_band_edges(padded, tile_id, tile_count):
    cycle_ids = jnp.arange(padded.shape[2], dtype=jnp.int32)
    at_start = (cycle_ids == 0) & (tile_id == 0)
    at_finish = (cycle_ids == padded.shape[2] - 1) & (tile_id == tile_count - 1)
    keeping = jnp.logical_not(at_start | at_finish)
    return jnp.where(keeping[None, None, :, None], padded, jnp.zeros_like(padded))


def unit(turns, period):
    angle = (turns % (2 * period)).astype(jnp.float32) * (math.pi / period)
    return jnp.cos(angle), -jnp.sin(angle)


def cycle_spectrum(rows, parity, pixels, orders):
    parts, n_r, n_x, pix = rows.shape
    count = pixels // LANES
    tops = orders // count
    a = jnp.arange(count, dtype=jnp.int32)
    m1 = jnp.arange(count, dtype=jnp.int32)
    k = jnp.arange(tops, dtype=jnp.int32)
    half = 2 * jnp.arange(LANES, dtype=jnp.int32)[None, :] + parity[:, None]
    first = jnp.stack(unit(2 * m1[:, None] * a[None, :], count))
    first = first.reshape(2, count, parts, pix // LANES)
    x = rows.reshape(parts, n_r, n_x, pix // LANES, LANES).astype(jnp.float32)
    y = jnp.einsum("zmfa,frxab->zmrxb", first, x, precision=lax.Precision.HIGHEST)
    tw_re, tw_im = unit(m1[:, None, None] * half[None], pixels)
    tw_re, tw_im = tw_re[:, :, None], tw_im[:, :, None]
    turned = jnp.stack([y[0] * tw_re - y[1] * tw_im, y[0] * tw_im + y[1] * tw_re])
    g_re, g_im = unit(half[:, :, None] * k[None, None, :], LANES)
    second = jnp.stack([jnp.stack([g_re, g_im]), jnp.stack([-g_im, g_re])])
    return jnp.einsum(
        "imrxb,izrbk->mkrzx", turned, second, precision=lax.Precision.HIGHEST
    ).astype(jnp.bfloat16)


def mix_body(slots, nz, sub, step, c_ref, q_ref, w_ref, o_ref, a_ref, t_ref):
    pk, pn, srcs, per, rr, ln = c_ref.shape
    depth = pk * rr
    count, ch = w_ref.shape[0], w_ref.shape[1]
    lane = lax.broadcasted_iota(jnp.int32, (1, ROWS, depth), 2)
    row = lax.broadcasted_iota(jnp.int32, (1, ROWS, depth), 1)
    own = (lane % ROWS) == row

    def associate(i, carry):
        held = []
        for h in range(2):
            g = 2 * i + h
            a, b = g // per, g % per
            rhs = [c_ref[:, n, a, b].reshape(depth, ln) for n in range(pn)]
            held.append((a, b, jnp.concatenate(rhs, axis=1)))
        for l0 in range(0, count, step):
            parts = []
            for a, b, rhs in held:
                q = q_ref[a, b, pl.ds(l0, step), :].astype(jnp.float32)
                d = jnp.where(own, q[:, None, :], 0.0).astype(jnp.bfloat16)
                r = jnp.dot(d.reshape(step * ROWS, depth), rhs, preferred_element_type=jnp.float32)
                parts.append(r.reshape(step, ROWS, nz * ch))
            both = jnp.concatenate(parts, axis=1).astype(jnp.bfloat16)
            a_ref[pl.ds(l0, step), pl.ds(pl.multiple_of(i * 2 * ROWS, 2 * ROWS), 2 * ROWS), :] = both
        return carry

    lax.fori_loop(0, srcs * per // 2, associate, 0)
    zero = jnp.zeros((sub, ch), jnp.bfloat16)

    def filtering(i, carry):
        for j in range(16):
            l = i * 16 + j
            w = w_ref[l]
            rows = []
            for c0 in range(0, ch, sub):
                for z in range(nz):
                    blocks = [w[c0 : c0 + sub] if y == z else zero for y in range(nz)]
                    rows.append(jnp.concatenate(blocks, axis=1))
            r = jnp.dot(a_ref[l], jnp.concatenate(rows, axis=0), preferred_element_type=jnp.float32)
            for z in range(nz):
                t_ref[z, pl.ds(j, slots, stride=16), :] = r[:, z * ch : (z + 1) * ch]
        for z in range(nz):
            o_ref[:, :, z, pl.ds(pl.multiple_of(i * 16, 16), 16), :] = (
                t_ref[z].reshape(srcs, per * ROWS, 16, ch).astype(jnp.bfloat16)
            )
        return carry

    lax.fori_loop(0, count // 16, filtering, 0)


def mix(coeffs, tables, weights, filled, chunk, chunks, sub):
    pk, pn, src, per, rr, ln = coeffs.shape
    _, _, count, depth = tables.shape
    ch = weights.shape[1]
    nz = pn * ln // ch
    srcs = max(1, min(src, LANES // (per * ROWS)))
    slots = srcs * per * ROWS
    body = functools.partial(mix_body, slots, nz, sub, min(16, count))
    in_specs = [
        pl.BlockSpec((pk, pn, srcs, per, rr, ln), lambda i: (0, 0, i, 0, 0, 0)),
        pl.BlockSpec((srcs, per, count, depth), lambda i: (i, 0, 0, 0)),
        pl.BlockSpec((count, ch, ch), lambda i: (0, 0, 0), pipeline_mode=pl.Buffered(1)),
    ]
    args = [coeffs, tables, weights]
    alias = {}
    run = body
    if filled is not None:
        in_specs.append(pl.BlockSpec(memory_space=pl.ANY))
        args.append(filled)
        alias = {3: 0}
        run = lambda c, q, w, p, o, a, t: body(c, q, w, o, a, t)
    size = src * per * ROWS * nz * count * ch
    return pl.pallas_call(
        run,
        grid=(src // srcs,),
        in_specs=in_specs,
        out_specs=pl.BlockSpec(
            (srcs, None, per * ROWS, nz, count, ch), lambda i: (i, chunk, 0, 0, 0, 0)
        ),
        out_shape=jax.ShapeDtypeStruct((src, chunks, per * ROWS, nz, count, ch), jnp.bfloat16),
        scratch_shapes=[
            pltpu.VMEM((count, slots, nz * ch), jnp.bfloat16),
            pltpu.VMEM((nz, slots * 16, ch), jnp.float32),
        ],
        input_output_aliases=alias,
        compiler_params=pltpu.CompilerParams(vmem_limit_bytes=60 << 20),
        cost_estimate=pl.CostEstimate(
            flops=size * 2 * (depth + nz * ch),
            transcendentals=0,
            bytes_accessed=2 * (coeffs.size + tables.size + weights.size + size),
        ),
        name="mix",
    )(*args)


def body(field, conv_weight, order_map, legendre, spectral_weight):
    n_chan = lax.axis_size("chan")
    n_face = lax.axis_size("face")
    n_tile = lax.axis_size("tile")
    chan_id = lax.axis_index("chan")
    face_id = lax.axis_index("face")
    tile_id = lax.axis_index("tile")
    samples, chan_dev, cycle_dev, pix_dev = field.shape
    pixels = pix_dev * n_face
    slot_dev, cycles, degrees = legendre.shape
    owners = n_face * n_tile
    degree_dev = degrees // owners
    n_cyc = math.gcd(n_face, cycle_dev)
    n_sub = n_face // n_cyc
    cyc_own = cycle_dev // n_cyc
    sub = chan_dev // n_sub
    groups = slot_dev // ROWS
    chunks = math.gcd(4, groups)
    per = groups // chunks

    slot_start = ((chan_id * n_face + face_id) * n_tile + tile_id) * slot_dev
    own_orders = lax.dynamic_slice_in_dim(order_map, slot_start, slot_dev)
    keeping = jnp.arange(degrees, dtype=jnp.int32)[None, :] >= own_orders[:, None]
    tables = jnp.where(keeping[:, None, :], legendre, jnp.zeros_like(legendre))
    tables = tables.reshape(
        chunks, per, ROWS, n_tile, n_cyc, cyc_own, owners, degree_dev
    ).transpose(0, 6, 1, 7, 4, 3, 5, 2)
    tables = tables.reshape(chunks, owners, per, degree_dev, cycles * ROWS)

    gathered = lax.all_gather(field, "chan", axis=1, tiled=True)
    padded = extended(gathered, (("face", 3), ("tile", 2)), 1)
    padded = clear_band_edges(padded, tile_id, n_tile)
    own_weight = lax.dynamic_slice_in_dim(conv_weight, chan_id * chan_dev, chan_dev, 3)
    hidden = stencil(padded, own_weight, cycle_dev, pix_dev).astype(jnp.bfloat16)
    hidden = hidden.reshape(samples, n_sub, sub, n_cyc, cyc_own, pix_dev)
    hidden = hidden.transpose(3, 1, 4, 0, 2, 5).reshape(n_face, cyc_own, samples * sub, pix_dev)
    hidden = lax.all_to_all(hidden, "face", split_axis=0, concat_axis=0, tiled=True)
    first_cycle = tile_id * cycle_dev + (face_id // n_sub) * cyc_own
    parity = (first_cycle + jnp.arange(cyc_own, dtype=jnp.int32)) % 2
    coeffs = cycle_spectrum(hidden, parity, pixels, degrees)
    tall = pixels // LANES
    coeffs = coeffs.reshape(degrees, cyc_own * 2 * samples * sub)
    place = (order_map % tall) * (degrees // tall) + order_map // tall
    picking = (place[:, None] == jnp.arange(degrees, dtype=jnp.int32)[None, :]).astype(jnp.bfloat16)
    coeffs = jnp.dot(picking, coeffs, preferred_element_type=jnp.float32).astype(jnp.bfloat16)
    width = 2 * samples * sub
    coeffs = coeffs.reshape(n_chan, owners, chunks, per, ROWS, cyc_own, width)
    coeffs = coeffs.transpose(0, 2, 1, 3, 5, 4, 6)
    coeffs = coeffs.reshape(n_chan, chunks, owners, per, cyc_own * ROWS, width)
    coeffs = lax.all_to_all(coeffs, "chan", split_axis=0, concat_axis=0, tiled=True)

    out = None
    for chunk in range(chunks):
        got = lax.all_gather(coeffs[:, chunk], ("face", "tile"), axis=0, tiled=False)
        if n_sub > 1:
            got = got.reshape(n_cyc, n_sub, n_tile, n_chan, owners, per, cyc_own * ROWS, width)
            got = got.transpose(0, 2, 3, 4, 5, 6, 1, 7)
        got = got.reshape(n_cyc * n_tile, n_chan, owners, per, cyc_own * ROWS, n_sub * width)
        table = lax.all_to_all(
            tables[chunk], ("face", "tile"), split_axis=0, concat_axis=0, tiled=True
        )
        out = mix(got, table, spectral_weight, out, chunk, chunks, sub)
    return out.reshape(owners * slot_dev, 2, samples, degree_dev, chan_dev * n_chan)


def solution(mesh):
    in_specs = (
        P(None, "chan", "tile", "face"),
        P(),
        P(),
        P(("chan", "face", "tile"), None, None),
        P(("face", "tile"), None, None),
    )
    out_specs = P("chan", None, None, ("face", "tile"), None)
    return jax.shard_map(body, mesh=mesh, in_specs=in_specs, out_specs=out_specs, check_vma=False)
```

```python
import functools
import math

import jax
import jax.numpy as jnp
import numpy as np
from jax import lax
from jax.experimental import pallas as pl
from jax.experimental.pallas import tpu as pltpu
from jax.sharding import PartitionSpec as P


LANES = 128
ROWS = 8
STRIDE = 17


def extended(field):
    n_face, n_tile = lax.axis_size("face"), lax.axis_size("tile")
    above = lax.ppermute(field[:, :, -1], "tile", [(i, i + 1) for i in range(n_tile - 1)])
    below = lax.ppermute(field[:, :, 0], "tile", [(i + 1, i) for i in range(n_tile - 1)])
    above, below = above[:, :, None], below[:, :, None]
    sides = []
    for pixel, step in ((-1, 1), (0, n_face - 1)):
        column = jnp.concatenate(
            [x[:, :, :, pixel] for x in (above, field, below)], axis=2
        ).transpose(0, 2, 1)
        pairs = [(i, (i + step) % n_face) for i in range(n_face)]
        column = lax.ppermute(column, "face", pairs)
        sides.append(column.transpose(0, 2, 1)[:, :, :, None])
    whole = jnp.concatenate([above, field, below], axis=2)
    return jnp.concatenate([sides[0], whole, sides[1]], axis=3)


def stencil(padded, weights, cycle_count, pix_count):
    summed = None
    for shift_r in range(3):
        for shift_p in range(3):
            window = padded[:, :, shift_r : shift_r + cycle_count, shift_p : shift_p + pix_count]
            contrib = jnp.einsum(
                "birp,io->borp",
                window,
                weights[shift_r, shift_p],
                preferred_element_type=jnp.float32,
            )
            summed = contrib if summed is None else summed + contrib
    return summed


def unit(turns, period):
    angle = (turns % (2 * period)).astype(jnp.float32) * (math.pi / period)
    return jnp.cos(angle), -jnp.sin(angle)


def cycle_spectrum(rows, pieces, parity, pixels, orders):
    parts, n_r, n_x, pix = rows.shape
    count = pixels // LANES
    tops = orders // count
    a = pieces[:, None] * (pix // LANES) + jnp.arange(pix // LANES, dtype=jnp.int32)[None, :]
    a = a.reshape(count)
    m1 = jnp.arange(count, dtype=jnp.int32)
    k = jnp.arange(tops, dtype=jnp.int32)
    half = 2 * jnp.arange(LANES, dtype=jnp.int32)[None, :] + parity[:, None]
    first = jnp.stack(unit(2 * m1[:, None] * a[None, :], count))
    first = first.reshape(2, count, parts, pix // LANES)
    x = rows.reshape(parts, n_r, n_x, pix // LANES, LANES).astype(jnp.float32)
    y = jnp.einsum("zmfa,frxab->zmrxb", first, x, precision=lax.Precision.HIGHEST)
    tw_re, tw_im = unit(m1[:, None, None] * half[None], pixels)
    tw_re, tw_im = tw_re[:, :, None], tw_im[:, :, None]
    turned = jnp.stack([y[0] * tw_re - y[1] * tw_im, y[0] * tw_im + y[1] * tw_re])
    g_re, g_im = unit(half[:, :, None] * k[None, None, :], LANES)
    second = jnp.stack([jnp.stack([g_re, g_im]), jnp.stack([-g_im, g_re])])
    return jnp.einsum(
        "imrxb,izrbk->rzmkx", turned, second, precision=lax.Precision.HIGHEST
    ).astype(jnp.bfloat16)


def table_body(n_tile, n_cyc, cyc_own, late, leg_ref, order_ref, *out_refs):
    _, count, depth = out_refs[0].shape
    cycles = depth // ROWS
    dest = pl.program_id(0)
    lanes = lax.broadcasted_iota(jnp.int32, (1, depth), 1)
    slot, rest = lanes % ROWS, lanes // ROWS
    cyc, rest = rest % cyc_own, rest // cyc_own
    rows = lax.broadcasted_iota(jnp.int32, (depth, depth), 0)

    def moving(back, part):
        tile = (dest % n_tile - back + n_tile) % n_tile
        source = slot * cycles + (tile * n_cyc + part) * cyc_own + cyc
        return jnp.where(rows == source, 1.0, 0.0).astype(jnp.bfloat16)

    usual = moving(rest % n_tile, rest // n_tile)
    other = moving(rest // n_cyc, rest % n_cyc)
    degree = dest * count + lax.broadcasted_iota(jnp.int32, (count, depth), 0)
    places = [(ref, i) for ref in out_refs for i in range(ref.shape[0])]
    for g, (ref, i) in enumerate(places):
        x = leg_ref[g * ROWS : (g + 1) * ROWS].reshape(depth, count)
        y = lax.dot_general(
            x,
            usual if g < late else other,
            (((0,), (0,)), ((), ())),
            preferred_element_type=jnp.float32,
        )
        ref[i] = jnp.where(degree >= order_ref[g], y, 0.0).astype(jnp.bfloat16)


def tables_for(legendre, orders, sizes, late, owners, n_tile, n_cyc, cyc_own):
    slots, cycles, degrees = legendre.shape
    count = degrees // owners
    groups = slots // ROWS
    depth = cycles * ROWS
    lane_orders = jnp.tile(orders.reshape(groups, 1, ROWS), (1, 1, cycles))
    return pl.pallas_call(
        functools.partial(table_body, n_tile, n_cyc, cyc_own, late),
        grid=(owners,),
        in_specs=[
            pl.BlockSpec((slots, cycles, count), lambda d: (0, 0, d)),
            pl.BlockSpec((groups, 1, depth), lambda d: (0, 0, 0)),
        ],
        out_specs=[
            pl.BlockSpec((None, n, count, depth), lambda d: (d, 0, 0, 0)) for n in sizes
        ],
        out_shape=[jax.ShapeDtypeStruct((owners, n, count, depth), jnp.bfloat16) for n in sizes],
        compiler_params=pltpu.CompilerParams(vmem_limit_bytes=24 << 20),
        cost_estimate=pl.CostEstimate(
            flops=2 * owners * groups * count * depth * depth,
            transcendentals=0,
            bytes_accessed=4 * owners * groups * count * depth,
        ),
        name="tables",
    )(legendre, lane_orders)


def plain_tables(legendre, orders, n_face, n_tile, n_cyc, cyc_own):
    slots, cycles, degrees = legendre.shape
    owners = n_face * n_tile
    per = slots // ROWS
    keeping = jnp.arange(degrees, dtype=jnp.int32)[None, :] >= orders[:, None]
    tables = jnp.where(keeping[:, None, :], legendre, jnp.zeros_like(legendre))
    tables = tables.reshape(
        per, ROWS, n_tile, n_cyc, cyc_own, n_face, n_tile, degrees // owners
    )
    turned = []
    for t in range(n_tile):
        back = [(t - k) % n_tile for k in range(n_tile)]
        turned.append(tables[:, :, jnp.array(back), :, :, :, t])
    tables = jnp.stack(turned, axis=6)
    tables = tables.transpose(5, 6, 0, 7, 3, 2, 4, 1)
    return tables.reshape(owners, per, degrees // owners, cycles * ROWS)


def partner(index, k, count):
    return index ^ k if count & (count - 1) == 0 else (k - index) % count


def swapped(blocks, axis):
    count = lax.axis_size(axis)
    index = lax.axis_index(axis)
    found = []
    for k in range(count):
        pairs = [(i, partner(i, k, count)) for i in range(count)]
        block = lax.dynamic_index_in_dim(blocks, partner(index, k, count), 0, keepdims=False)
        moves = any(i != j for i, j in pairs)
        found.append(lax.ppermute(block, axis, pairs) if moves else block)
    return jnp.stack(found)


def along_tiles(piece):
    n_tile = lax.axis_size("tile")
    tile_id = lax.axis_index("tile")
    up = [(i, i + 1) for i in range(n_tile - 1)]
    down = [(i + 1, i) for i in range(n_tile - 1)]
    rising, falling = [piece], [piece]
    for _ in range(n_tile - 1):
        rising.append(lax.ppermute(rising[-1], "tile", up))
        falling.append(lax.ppermute(falling[-1], "tile", down))
    parts = [piece]
    for k in range(1, n_tile):
        parts.append(jnp.where(tile_id >= k, rising[k], falling[n_tile - k]))
    return jnp.stack(parts)


def mix_body(slots, nz, sub, step, c_ref, w_ref, *refs):
    *q_refs, o_ref, a_ref, t_ref = refs
    pk, pn, srcs, per, rr, ln = c_ref.shape
    depth = pk * rr
    count, ch = w_ref.shape[0], w_ref.shape[1]
    lane = lax.broadcasted_iota(jnp.int32, (1, ROWS, depth), 2)
    row = lax.broadcasted_iota(jnp.int32, (1, ROWS, depth), 1)
    own = (lane % ROWS) == row

    def associate(i, carry):
        held = []
        for h in range(2):
            a, b = (i, h) if per == 2 else ((2 * i + h) // per, (2 * i + h) % per)
            rhs = [c_ref[:, n, a, b].reshape(depth, ln) for n in range(pn)]
            held.append((a, b, jnp.concatenate(rhs, axis=1)))
        for l0 in range(0, count, step):
            parts = []
            for a, b, rhs in held:
                q_ref, at = (q_refs[0], b) if len(q_refs) == 1 else (q_refs[b], 0)
                q = q_ref[a, at, pl.ds(l0, step), :].astype(jnp.float32)
                d = jnp.where(own, q[:, None, :], 0.0).astype(jnp.bfloat16)
                r = jnp.dot(d.reshape(step * ROWS, depth), rhs, preferred_element_type=jnp.float32)
                parts.append(r.reshape(step, ROWS, nz * ch))
            both = jnp.concatenate(parts, axis=1).astype(jnp.bfloat16)
            a_ref[pl.ds(l0, step), pl.ds(pl.multiple_of(i * 2 * ROWS, 2 * ROWS), 2 * ROWS), :] = both
        return carry

    lax.fori_loop(0, srcs * per // 2, associate, 0)
    zero = jnp.zeros((sub, ch), jnp.bfloat16)

    def filtering(i, carry):
        for j in range(16):
            l = i * 16 + j
            w = w_ref[l]
            rows = []
            for c0 in range(0, ch, sub):
                for z in range(nz):
                    blocks = [w[c0 : c0 + sub] if y == z else zero for y in range(nz)]
                    rows.append(jnp.concatenate(blocks, axis=1))
            r = jnp.dot(a_ref[l], jnp.concatenate(rows, axis=0), preferred_element_type=jnp.float32)
            for z in range(nz):
                t_ref[z, pl.ds(j, slots, stride=STRIDE), :] = r[:, z * ch : (z + 1) * ch]
        at = pl.ds(pl.multiple_of(i * 16, 16), 16)
        for z in range(nz):
            for x in range(slots):
                o_ref[x // (per * ROWS), x % (per * ROWS), z, at, :] = t_ref[
                    z, pl.ds(x * STRIDE, 16), :
                ].astype(jnp.bfloat16)
        return carry

    lax.fori_loop(0, count // 16, filtering, 0)


def mix(coeffs, tables, weights, filled, chunk, chunks, sub):
    pk, pn, src, per, rr, ln = coeffs.shape
    count, depth = tables[0].shape[2:]
    ch = weights.shape[1]
    nz = pn * ln // ch
    srcs = max(1, min(src, LANES // (per * ROWS)))
    slots = srcs * per * ROWS
    body = functools.partial(mix_body, slots, nz, sub, min(16, count))
    in_specs = [
        pl.BlockSpec((pk, pn, srcs, per, rr, ln), lambda i: (0, 0, i, 0, 0, 0)),
        pl.BlockSpec((count, ch, ch), lambda i: (0, 0, 0), pipeline_mode=pl.Buffered(1)),
    ]
    for table in tables:
        in_specs.append(pl.BlockSpec((srcs, table.shape[1], count, depth), lambda i: (i, 0, 0, 0)))
    args = [coeffs, weights, *tables]
    alias = {}
    run = body
    if filled is not None:
        alias = {len(args): 0}
        in_specs.append(pl.BlockSpec(memory_space=pl.ANY))
        args.append(filled)
        run = lambda *refs: body(*refs[: len(args) - 1], *refs[len(args) :])
    size = src * per * ROWS * nz * count * ch
    return pl.pallas_call(
        run,
        grid=(src // srcs,),
        in_specs=in_specs,
        out_specs=pl.BlockSpec(
            (srcs, None, per * ROWS, nz, count, ch), lambda i: (i, chunk, 0, 0, 0, 0)
        ),
        out_shape=jax.ShapeDtypeStruct((src, chunks, per * ROWS, nz, count, ch), jnp.bfloat16),
        scratch_shapes=[
            pltpu.VMEM((count, slots, nz * ch), jnp.bfloat16),
            pltpu.VMEM((nz, slots * STRIDE, ch), jnp.float32),
        ],
        input_output_aliases=alias,
        compiler_params=pltpu.CompilerParams(vmem_limit_bytes=60 << 20),
        cost_estimate=pl.CostEstimate(
            flops=size * 2 * (depth + nz * ch),
            transcendentals=0,
            bytes_accessed=2 * (coeffs.size + sum(t.size for t in tables) + weights.size + size),
        ),
        name="mix",
    )(*args)


def body(field, conv_weight, order_map, legendre, spectral_weight):
    n_chan = lax.axis_size("chan")
    n_face = lax.axis_size("face")
    n_tile = lax.axis_size("tile")
    chan_id = lax.axis_index("chan")
    face_id = lax.axis_index("face")
    tile_id = lax.axis_index("tile")
    samples, chan_dev, cycle_dev, pix_dev = field.shape
    pixels = pix_dev * n_face
    slot_dev, _, degrees = legendre.shape
    owners = n_face * n_tile
    degree_dev = degrees // owners
    n_cyc = math.gcd(n_face, cycle_dev)
    n_sub = n_face // n_cyc
    cyc_own = cycle_dev // n_cyc
    sub = chan_dev // n_sub
    groups = slot_dev // ROWS
    per = math.gcd(2, groups)
    chunks = groups // per
    sizes = [[1] * per if c == 1 else [per] for c in range(chunks)]
    late = chunks - 1 if chunks > 2 and n_sub == 1 and degree_dev >= LANES else chunks

    slot_start = ((chan_id * n_face + face_id) * n_tile + tile_id) * slot_dev
    own_orders = lax.dynamic_slice_in_dim(order_map, slot_start, slot_dev)
    if degree_dev >= LANES:
        tables = tables_for(legendre, own_orders, sum(sizes, []), late * per, owners, n_tile, n_cyc, cyc_own)
    else:
        tables = plain_tables(legendre, own_orders, n_face, n_tile, n_cyc, cyc_own)
        tables = jnp.split(tables, list(np.cumsum(sum(sizes, []))[:-1]), axis=1)
    weights = jnp.roll(spectral_weight, -chan_id * chan_dev, axis=1)

    padded = extended(field)
    padded = lax.all_gather(padded, "chan", axis=1, tiled=True)

    fetched = []
    tables = list(tables)
    for c in range(chunks):
        parts = []
        for _ in range(len(sizes[c])):
            parts.append(
                lax.all_to_all(
                    tables.pop(0), ("face", "tile"), split_axis=0, concat_axis=0, tiled=True
                )
            )
        fetched.append(parts)
    own_weight = lax.dynamic_slice_in_dim(conv_weight, chan_id * chan_dev, chan_dev, 3)
    hidden = stencil(padded, own_weight, cycle_dev, pix_dev).astype(jnp.bfloat16)
    hidden = hidden.reshape(samples, n_sub, sub, n_cyc, cyc_own, pix_dev)
    hidden = hidden.transpose(3, 1, 4, 0, 2, 5).reshape(n_face, cyc_own, samples * sub, pix_dev)
    hidden = swapped(hidden, "face")
    pieces = partner(face_id, jnp.arange(n_face, dtype=jnp.int32), n_face)
    first_cycle = tile_id * cycle_dev + (face_id // n_sub) * cyc_own
    parity = (first_cycle + jnp.arange(cyc_own, dtype=jnp.int32)) % 2
    coeffs = cycle_spectrum(hidden, pieces, parity, pixels, degrees)
    tall = pixels // LANES
    coeffs = coeffs.reshape(cyc_own * 2, degrees, samples * sub)
    coeffs = jnp.concatenate(list(coeffs), axis=1)
    order_map = jnp.roll(order_map, -chan_id * owners * slot_dev)
    place = (order_map % tall) * (degrees // tall) + order_map // tall
    picking = (place[:, None] == jnp.arange(degrees, dtype=jnp.int32)[None, :]).astype(jnp.bfloat16)
    coeffs = jnp.dot(picking, coeffs, preferred_element_type=jnp.float32).astype(jnp.bfloat16)
    width = 2 * samples * sub
    coeffs = coeffs.reshape(n_chan, owners, chunks, per, ROWS, cyc_own, width)
    coeffs = coeffs.transpose(0, 2, 1, 3, 5, 4, 6)
    coeffs = coeffs.reshape(n_chan, chunks, owners, per, cyc_own * ROWS, width)
    turns = [coeffs[0]]
    for k in range(1, n_chan):
        pairs = [((i + k) % n_chan, i) for i in range(n_chan)]
        turns.append(lax.ppermute(coeffs[n_chan - k], "chan", pairs))
    coeffs = jnp.stack(turns)

    if late < chunks:
        across = lax.all_gather(coeffs[:, late], "face", axis=0, tiled=False)
    lines = [along_tiles(coeffs[:, :1])]
    if chunks > 1:
        lines.append(along_tiles(coeffs[:, 1:late]))
    out = None
    for chunk in range(chunks):
        if chunk == late:
            got = along_tiles(across)
        else:
            line = lines[0][:, :, 0] if chunk == 0 else lines[1][:, :, chunk - 1]
            got = lax.all_gather(line, "face", axis=0, tiled=False)
        if n_sub > 1:
            got = got.reshape(n_cyc, n_sub, n_tile, n_chan, owners, per, cyc_own * ROWS, width)
            got = got.transpose(0, 2, 3, 4, 5, 6, 1, 7)
        got = got.reshape(n_cyc * n_tile, n_chan, owners, per, cyc_own * ROWS, n_sub * width)
        out = mix(got, fetched[chunk], weights, out, chunk, chunks, sub)
    return out.reshape(owners * slot_dev, 2, samples, degree_dev, chan_dev * n_chan)


def solution(mesh):
    in_specs = (
        P(None, "chan", "tile", "face"),
        P(),
        P(),
        P(("chan", "face", "tile"), None, None),
        P(("face", "tile"), None, None),
    )
    out_specs = P("chan", None, None, ("face", "tile"), None)
    return jax.shard_map(body, mesh=mesh, in_specs=in_specs, out_specs=out_specs, check_vma=False)
```

```python
import functools
import math

import jax
import jax.numpy as jnp
import numpy as np
from jax import lax
from jax.experimental import pallas as pl
from jax.experimental.pallas import tpu as pltpu
from jax.sharding import PartitionSpec as P


LANES = 128
ROWS = 8
STRIDE = 17


def extended(field):
    n_face, n_tile = lax.axis_size("face"), lax.axis_size("tile")
    above = lax.ppermute(field[:, :, -1], "tile", [(i, i + 1) for i in range(n_tile - 1)])
    below = lax.ppermute(field[:, :, 0], "tile", [(i + 1, i) for i in range(n_tile - 1)])
    above, below = above[:, :, None], below[:, :, None]
    sides = []
    for pixel, step in ((-1, 1), (0, n_face - 1)):
        column = jnp.concatenate(
            [x[:, :, :, pixel] for x in (above, field, below)], axis=2
        ).transpose(0, 2, 1)
        pairs = [(i, (i + step) % n_face) for i in range(n_face)]
        column = lax.ppermute(column, "face", pairs)
        sides.append(column.transpose(0, 2, 1)[:, :, :, None])
    whole = jnp.concatenate([above, field, below], axis=2)
    return jnp.concatenate([sides[0], whole, sides[1]], axis=3)


def stencil(padded, weights, cycle_count, pix_count):
    summed = None
    for shift_r in range(3):
        for shift_p in range(3):
            window = padded[:, :, shift_r : shift_r + cycle_count, shift_p : shift_p + pix_count]
            contrib = jnp.einsum(
                "birp,io->borp",
                window,
                weights[shift_r, shift_p],
                preferred_element_type=jnp.float32,
            )
            summed = contrib if summed is None else summed + contrib
    return summed


def unit(turns, period):
    angle = (turns % (2 * period)).astype(jnp.float32) * (math.pi / period)
    return jnp.cos(angle), -jnp.sin(angle)


def cycle_spectrum(rows, pieces, parity, pixels, orders):
    parts, n_r, n_x, pix = rows.shape
    count = pixels // LANES
    tops = orders // count
    a = pieces[:, None] * (pix // LANES) + jnp.arange(pix // LANES, dtype=jnp.int32)[None, :]
    a = a.reshape(count)
    m1 = jnp.arange(count, dtype=jnp.int32)
    k = jnp.arange(tops, dtype=jnp.int32)
    half = 2 * jnp.arange(LANES, dtype=jnp.int32)[None, :] + parity[:, None]
    first = jnp.stack(unit(2 * m1[:, None] * a[None, :], count))
    first = first.reshape(2, count, parts, pix // LANES)
    x = rows.reshape(parts, n_r, n_x, pix // LANES, LANES).astype(jnp.float32)
    y = jnp.einsum("zmfa,frxab->zmrxb", first, x, precision=lax.Precision.HIGHEST)
    tw_re, tw_im = unit(m1[:, None, None] * half[None], pixels)
    tw_re, tw_im = tw_re[:, :, None], tw_im[:, :, None]
    turned = jnp.stack([y[0] * tw_re - y[1] * tw_im, y[0] * tw_im + y[1] * tw_re])
    g_re, g_im = unit(half[:, :, None] * k[None, None, :], LANES)
    second = jnp.stack([jnp.stack([g_re, g_im]), jnp.stack([-g_im, g_re])])
    return jnp.einsum(
        "imrxb,izrbk->rzmkx", turned, second, precision=lax.Precision.HIGHEST
    ).astype(jnp.bfloat16)


def table_body(n_tile, n_cyc, cyc_own, late, leg_ref, order_ref, *out_refs):
    _, count, depth = out_refs[0].shape
    cycles = depth // ROWS
    dest = pl.program_id(0)
    lanes = lax.broadcasted_iota(jnp.int32, (1, depth), 1)
    slot, rest = lanes % ROWS, lanes // ROWS
    cyc, rest = rest % cyc_own, rest // cyc_own
    rows = lax.broadcasted_iota(jnp.int32, (depth, depth), 0)

    def moving(back, part):
        tile = (dest % n_tile - back + n_tile) % n_tile
        source = slot * cycles + (tile * n_cyc + part) * cyc_own + cyc
        return jnp.where(rows == source, 1.0, 0.0).astype(jnp.bfloat16)

    usual = moving(rest % n_tile, rest // n_tile)
    other = moving(rest // n_cyc, rest % n_cyc)
    degree = dest * count + lax.broadcasted_iota(jnp.int32, (count, depth), 0)
    places = [(ref, i) for ref in out_refs for i in range(ref.shape[0])]
    for g, (ref, i) in enumerate(places):
        x = leg_ref[g * ROWS : (g + 1) * ROWS].reshape(depth, count)
        y = lax.dot_general(
            x,
            usual if g < late else other,
            (((0,), (0,)), ((), ())),
            preferred_element_type=jnp.float32,
        )
        ref[i] = jnp.where(degree >= order_ref[g], y, 0.0).astype(jnp.bfloat16)


def tables_for(legendre, orders, sizes, late, owners, n_tile, n_cyc, cyc_own):
    slots, cycles, degrees = legendre.shape
    count = degrees // owners
    groups = slots // ROWS
    depth = cycles * ROWS
    lane_orders = jnp.tile(orders.reshape(groups, 1, ROWS), (1, 1, cycles))
    return pl.pallas_call(
        functools.partial(table_body, n_tile, n_cyc, cyc_own, late),
        grid=(owners,),
        in_specs=[
            pl.BlockSpec((slots, cycles, count), lambda d: (0, 0, d)),
            pl.BlockSpec((groups, 1, depth), lambda d: (0, 0, 0)),
        ],
        out_specs=[
            pl.BlockSpec((None, n, count, depth), lambda d: (d, 0, 0, 0)) for n in sizes
        ],
        out_shape=[jax.ShapeDtypeStruct((owners, n, count, depth), jnp.bfloat16) for n in sizes],
        compiler_params=pltpu.CompilerParams(vmem_limit_bytes=24 << 20),
        cost_estimate=pl.CostEstimate(
            flops=2 * owners * groups * count * depth * depth,
            transcendentals=0,
            bytes_accessed=4 * owners * groups * count * depth,
        ),
        name="tables",
    )(legendre, lane_orders)


def plain_tables(legendre, orders, n_face, n_tile, n_cyc, cyc_own):
    slots, cycles, degrees = legendre.shape
    owners = n_face * n_tile
    per = slots // ROWS
    keeping = jnp.arange(degrees, dtype=jnp.int32)[None, :] >= orders[:, None]
    tables = jnp.where(keeping[:, None, :], legendre, jnp.zeros_like(legendre))
    tables = tables.reshape(
        per, ROWS, n_tile, n_cyc, cyc_own, n_face, n_tile, degrees // owners
    )
    turned = []
    for t in range(n_tile):
        back = [(t - k) % n_tile for k in range(n_tile)]
        turned.append(tables[:, :, jnp.array(back), :, :, :, t])
    tables = jnp.stack(turned, axis=6)
    tables = tables.transpose(5, 6, 0, 7, 3, 2, 4, 1)
    return tables.reshape(owners, per, degrees // owners, cycles * ROWS)


def partner(index, k, count):
    return index ^ k if count & (count - 1) == 0 else (k - index) % count


def swapped(blocks, axis):
    count = lax.axis_size(axis)
    index = lax.axis_index(axis)
    found = []
    for k in range(count):
        pairs = [(i, partner(i, k, count)) for i in range(count)]
        block = lax.dynamic_index_in_dim(blocks, partner(index, k, count), 0, keepdims=False)
        moves = any(i != j for i, j in pairs)
        found.append(lax.ppermute(block, axis, pairs) if moves else block)
    return jnp.stack(found)


def along_tiles(piece):
    n_tile = lax.axis_size("tile")
    tile_id = lax.axis_index("tile")
    up = [(i, i + 1) for i in range(n_tile - 1)]
    down = [(i + 1, i) for i in range(n_tile - 1)]
    rising, falling = [piece], [piece]
    for _ in range(n_tile - 2):
        rising.append(lax.ppermute(rising[-1], "tile", up))
        falling.append(lax.ppermute(falling[-1], "tile", down))
    ends = lax.ppermute(piece, "tile", [(0, n_tile - 1), (n_tile - 1, 0)])
    rising.append(ends)
    falling.append(ends)
    parts = [piece]
    for k in range(1, n_tile):
        parts.append(jnp.where(tile_id >= k, rising[k], falling[n_tile - k]))
    return jnp.stack(parts)


def around_tiles(piece):
    n_tile = lax.axis_size("tile")
    parts = [piece]
    for k in range(1, n_tile):
        parts.append(lax.ppermute(piece, "tile", [(i, (i + k) % n_tile) for i in range(n_tile)]))
    return jnp.stack(parts)


def mix_body(slots, nz, sub, step, c_ref, w_ref, *refs):
    *q_refs, o_ref, a_ref, t_ref = refs
    pk, pn, srcs, per, rr, ln = c_ref.shape
    depth = pk * rr
    count, ch = w_ref.shape[0], w_ref.shape[1]
    lane = lax.broadcasted_iota(jnp.int32, (1, ROWS, depth), 2)
    row = lax.broadcasted_iota(jnp.int32, (1, ROWS, depth), 1)
    own = (lane % ROWS) == row

    def associate(i, carry):
        held = []
        for h in range(2):
            a, b = (i, h) if per == 2 else ((2 * i + h) // per, (2 * i + h) % per)
            rhs = [c_ref[:, n, a, b].reshape(depth, ln) for n in range(pn)]
            held.append((a, b, jnp.concatenate(rhs, axis=1)))
        for l0 in range(0, count, step):
            parts = []
            for a, b, rhs in held:
                q_ref, at = (q_refs[0], b) if len(q_refs) == 1 else (q_refs[b], 0)
                q = q_ref[a, at, pl.ds(l0, step), :].astype(jnp.float32)
                d = jnp.where(own, q[:, None, :], 0.0).astype(jnp.bfloat16)
                r = jnp.dot(d.reshape(step * ROWS, depth), rhs, preferred_element_type=jnp.float32)
                parts.append(r.reshape(step, ROWS, nz * ch))
            both = jnp.concatenate(parts, axis=1).astype(jnp.bfloat16)
            a_ref[pl.ds(l0, step), pl.ds(pl.multiple_of(i * 2 * ROWS, 2 * ROWS), 2 * ROWS), :] = both
        return carry

    lax.fori_loop(0, srcs * per // 2, associate, 0)
    zero = jnp.zeros((sub, ch), jnp.bfloat16)

    def filtering(i, carry):
        for j in range(16):
            l = i * 16 + j
            w = w_ref[l]
            rows = []
            for c0 in range(0, ch, sub):
                for z in range(nz):
                    blocks = [w[c0 : c0 + sub] if y == z else zero for y in range(nz)]
                    rows.append(jnp.concatenate(blocks, axis=1))
            r = jnp.dot(a_ref[l], jnp.concatenate(rows, axis=0), preferred_element_type=jnp.float32)
            for z in range(nz):
                t_ref[z, pl.ds(j, slots, stride=STRIDE), :] = r[:, z * ch : (z + 1) * ch]
        at = pl.ds(pl.multiple_of(i * 16, 16), 16)
        for z in range(nz):
            for x in range(slots):
                o_ref[x // (per * ROWS), x % (per * ROWS), z, at, :] = t_ref[
                    z, pl.ds(x * STRIDE, 16), :
                ].astype(jnp.bfloat16)
        return carry

    lax.fori_loop(0, count // 16, filtering, 0)


def mix(coeffs, tables, weights, filled, chunk, chunks, sub):
    pk, pn, src, per, rr, ln = coeffs.shape
    count, depth = tables[0].shape[2:]
    ch = weights.shape[1]
    nz = pn * ln // ch
    srcs = max(1, min(src, LANES // (per * ROWS)))
    slots = srcs * per * ROWS
    body = functools.partial(mix_body, slots, nz, sub, min(16, count))
    in_specs = [
        pl.BlockSpec((pk, pn, srcs, per, rr, ln), lambda i: (0, 0, i, 0, 0, 0)),
        pl.BlockSpec((count, ch, ch), lambda i: (0, 0, 0), pipeline_mode=pl.Buffered(1)),
    ]
    for table in tables:
        in_specs.append(pl.BlockSpec((srcs, table.shape[1], count, depth), lambda i: (i, 0, 0, 0)))
    args = [coeffs, weights, *tables]
    alias = {}
    run = body
    if filled is not None:
        alias = {len(args): 0}
        in_specs.append(pl.BlockSpec(memory_space=pl.ANY))
        args.append(filled)
        run = lambda *refs: body(*refs[: len(args) - 1], *refs[len(args) :])
    size = src * per * ROWS * nz * count * ch
    return pl.pallas_call(
        run,
        grid=(src // srcs,),
        in_specs=in_specs,
        out_specs=pl.BlockSpec(
            (srcs, None, per * ROWS, nz, count, ch), lambda i: (i, chunk, 0, 0, 0, 0)
        ),
        out_shape=jax.ShapeDtypeStruct((src, chunks, per * ROWS, nz, count, ch), jnp.bfloat16),
        scratch_shapes=[
            pltpu.VMEM((count, slots, nz * ch), jnp.bfloat16),
            pltpu.VMEM((nz, slots * STRIDE, ch), jnp.float32),
        ],
        input_output_aliases=alias,
        compiler_params=pltpu.CompilerParams(vmem_limit_bytes=60 << 20),
        cost_estimate=pl.CostEstimate(
            flops=size * 2 * (depth + nz * ch),
            transcendentals=0,
            bytes_accessed=2 * (coeffs.size + sum(t.size for t in tables) + weights.size + size),
        ),
        name="mix",
    )(*args)


def body(field, conv_weight, order_map, legendre, spectral_weight):
    n_chan = lax.axis_size("chan")
    n_face = lax.axis_size("face")
    n_tile = lax.axis_size("tile")
    chan_id = lax.axis_index("chan")
    face_id = lax.axis_index("face")
    tile_id = lax.axis_index("tile")
    samples, chan_dev, cycle_dev, pix_dev = field.shape
    pixels = pix_dev * n_face
    slot_dev, _, degrees = legendre.shape
    owners = n_face * n_tile
    degree_dev = degrees // owners
    n_cyc = math.gcd(n_face, cycle_dev)
    n_sub = n_face // n_cyc
    cyc_own = cycle_dev // n_cyc
    sub = chan_dev // n_sub
    groups = slot_dev // ROWS
    per = math.gcd(2, groups)
    chunks = groups // per
    sizes = [[1] * per if c == 1 else [per] for c in range(chunks)]
    late = chunks - 1 if chunks > 2 and n_sub == 1 and degree_dev >= LANES else chunks

    slot_start = ((chan_id * n_face + face_id) * n_tile + tile_id) * slot_dev
    own_orders = lax.dynamic_slice_in_dim(order_map, slot_start, slot_dev)
    if degree_dev >= LANES:
        tables = tables_for(legendre, own_orders, sum(sizes, []), late * per, owners, n_tile, n_cyc, cyc_own)
    else:
        tables = plain_tables(legendre, own_orders, n_face, n_tile, n_cyc, cyc_own)
        tables = jnp.split(tables, list(np.cumsum(sum(sizes, []))[:-1]), axis=1)

    padded = extended(field)
    padded = lax.all_gather(padded, "chan", axis=1, tiled=True)
    weights = jnp.roll(spectral_weight, -chan_id * chan_dev, axis=1)

    fetched = []
    tables = list(tables)
    for c in range(chunks):
        parts = []
        for _ in range(len(sizes[c])):
            parts.append(
                lax.all_to_all(
                    tables.pop(0), ("face", "tile"), split_axis=0, concat_axis=0, tiled=True
                )
            )
        fetched.append(parts)
    own_weight = lax.dynamic_slice_in_dim(conv_weight, chan_id * chan_dev, chan_dev, 3)
    hidden = stencil(padded, own_weight, cycle_dev, pix_dev).astype(jnp.bfloat16)
    hidden = hidden.reshape(samples, n_sub, sub, n_cyc, cyc_own, pix_dev)
    hidden = hidden.transpose(3, 1, 4, 0, 2, 5).reshape(n_face, cyc_own, samples * sub, pix_dev)
    hidden = swapped(hidden, "face")
    pieces = partner(face_id, jnp.arange(n_face, dtype=jnp.int32), n_face)
    first_cycle = tile_id * cycle_dev + (face_id // n_sub) * cyc_own
    parity = (first_cycle + jnp.arange(cyc_own, dtype=jnp.int32)) % 2
    coeffs = cycle_spectrum(hidden, pieces, parity, pixels, degrees)
    tall = pixels // LANES
    coeffs = coeffs.reshape(cyc_own * 2, degrees, samples * sub)
    coeffs = jnp.concatenate(list(coeffs), axis=1)
    order_map = jnp.roll(order_map, -chan_id * owners * slot_dev)
    place = (order_map % tall) * (degrees // tall) + order_map // tall
    picking = (place[:, None] == jnp.arange(degrees, dtype=jnp.int32)[None, :]).astype(jnp.bfloat16)
    coeffs = jnp.dot(picking, coeffs, preferred_element_type=jnp.float32).astype(jnp.bfloat16)
    width = 2 * samples * sub
    coeffs = coeffs.reshape(n_chan, owners, chunks, per, ROWS, cyc_own, width)
    coeffs = coeffs.transpose(0, 2, 1, 3, 5, 4, 6)
    coeffs = coeffs.reshape(n_chan, chunks, owners, per, cyc_own * ROWS, width)
    turns = [coeffs[0]]
    for k in range(1, n_chan):
        pairs = [((i + k) % n_chan, i) for i in range(n_chan)]
        turns.append(lax.ppermute(coeffs[n_chan - k], "chan", pairs))
    coeffs = jnp.stack(turns)

    if late < chunks:
        across = lax.all_gather(coeffs[:, late], "face", axis=0, tiled=False)
    lines = [around_tiles(coeffs[:, :1])]
    if chunks > 1:
        lines.append(along_tiles(coeffs[:, 1:late]))
    out = None
    for chunk in range(chunks):
        if chunk == late:
            got = along_tiles(across)
        else:
            line = lines[0][:, :, 0] if chunk == 0 else lines[1][:, :, chunk - 1]
            got = lax.all_gather(line, "face", axis=0, tiled=False)
        if n_sub > 1:
            got = got.reshape(n_cyc, n_sub, n_tile, n_chan, owners, per, cyc_own * ROWS, width)
            got = got.transpose(0, 2, 3, 4, 5, 6, 1, 7)
        got = got.reshape(n_cyc * n_tile, n_chan, owners, per, cyc_own * ROWS, n_sub * width)
        out = mix(got, fetched[chunk], weights, out, chunk, chunks, sub)
    return out.reshape(owners * slot_dev, 2, samples, degree_dev, chan_dev * n_chan)


def solution(mesh):
    in_specs = (
        P(None, "chan", "tile", "face"),
        P(),
        P(),
        P(("chan", "face", "tile"), None, None),
        P(("face", "tile"), None, None),
    )
    out_specs = P("chan", None, None, ("face", "tile"), None)
    return jax.shard_map(body, mesh=mesh, in_specs=in_specs, out_specs=out_specs, check_vma=False)
```
